128 devices in a mesh: row: 8 (over x, y_lo), col: 16 (over y_hi, z, core).
Axes of the slice: x: 4, y: 4 (y_hi: 2, y_lo: 2; y = y_hi * 2 + y_lo), z: 4, core: 2. Of those that a mesh axis runs over, the one named last changes fastest.
Arguments:
- multiplier: float32 [512, 20480], P(('row', 'col')), may hold values from -6 to 6
- cycle_tiles: float32 [20480, 512], P('row', 'col'), may hold values from -0.0625 to 0.0625
Outputs:
- symmetric: float32 [512, 512], P(('row', 'col'))
The draws below stay inside these ranges and needn't reach their ends.
All inputs are finite; a program needn't handle non-finite values.
Results may differ from the reference program's by a relative error of at most 0.00007.
Values sent between devices are 32-bit elements; how exact they have to be, the bound alone decides.
No kernel may reach another device: no remote copies, remote signals or barrier semaphores. Data moves between devices by JAX's collectives and lax.ppermute only.
A program may use at most 64 MiB of HBM per device.

```python
import jax
import jax.numpy as jnp
from jax import lax

O = 40
V = 512
OW = 1
ROWS = 512
JW = 512
K = 20480
N_ROW = 8
N_COL = 16


def with_spikes(drawn, rng, source, target, shards_of, factor):
    owner, partner = [(jnp.arange(drawn.shape[dim]) // (drawn.shape[dim] // shards_of)).reshape([-1 if axis == dim else 1 for axis in range(drawn.ndim)]) for dim in (source, target)]
    chosen = jax.random.permutation(rng, shards_of)[partner]
    strong = (owner == chosen) | (owner == (partner + shards_of // 2) % shards_of)
    return jnp.where(strong, factor * drawn, drawn)


def block_levels(rng, dims, shards, least, largest):
    loudness = 1.0
    for position, parts in shards:
        draws = jax.random.uniform(jax.random.fold_in(jax.random.fold_in(rng, 6), position), (parts,), jnp.float32, least / len(shards), largest / len(shards))
        loudness = loudness * jnp.repeat(jnp.exp(draws), dims[position] // parts).reshape((-1,) + (1,) * (len(dims) - 1 - position))
    return loudness


def noise(key, extent, scale, reach, cuts=(), dtype=jnp.bfloat16):
    entries = jax.random.normal(key, extent, jnp.float32) * scale
    if len(cuts) > 0:
        entries = block_levels(key, extent, cuts, -0.22, 0.18) * entries
    return jnp.clip(entries, min=-reach, max=reach).astype(dtype)


def heavy_noise(own_key, extent, width, reach, pieces, heavy, held_as=jnp.bfloat16):
    result = width * jax.random.normal(own_key, extent, jnp.float32)
    if pieces:
        result = result * block_levels(own_key, extent, pieces, -0.22, 0.18)
    return jnp.clip(with_spikes(result, jax.random.fold_in(own_key, 3), *heavy), -reach, reach).astype(held_as)


def setup_inputs(seed: int = 0) -> dict:
    seeds = jax.random.split(jax.random.key(seed), 3)
    multiplier = noise(seeds[0], (ROWS, K), 1.0, 6.0, ((0, 128),), jnp.float32)
    cycle_tiles = heavy_noise(seeds[1], (K, JW), K ** -0.5, 0.0625, ((0, 8), (1, 16)), (0, 1, 16, 2.0), jnp.float32)
    return dict(multiplier=multiplier, cycle_tiles=cycle_tiles)


def reference(multiplier, cycle_tiles):
    block_width = JW // (N_ROW * N_COL)
    cycle_full = jnp.transpose(cycle_tiles.reshape(K, N_COL, N_ROW, block_width), (0, 2, 1, 3)).reshape(K, JW)
    swapped = jnp.transpose(multiplier.reshape(V, OW, V, O), (2, 1, 0, 3)).reshape(ROWS, K)
    combined = 2.0 * multiplier - swapped
    cycle_term = jnp.dot(combined, cycle_full, precision=lax.Precision.HIGHEST, preferred_element_type=jnp.float32)
    mirror = jnp.transpose(cycle_term.reshape(V, OW, V, OW), (2, 1, 0, 3)).reshape(ROWS, JW)
    return cycle_term + mirror
```

```python
import jax
import jax.numpy as jnp
from jax import lax
from jax.experimental import pallas as pl
from jax.experimental.pallas import tpu as pltpu
from jax.sharding import PartitionSpec as P

O = 40
V = 512
LANES = 128
PER = 4
DEPTH = PER * O
REST = DEPTH - LANES
DEVICES = V // PER
ROWS_OUT = PER * V // LANES

VMEM = pltpu.VMEM
F32 = jnp.float32


def call(body, out_shapes, scratch=(), flops=0, moved=1 << 20):
    several = isinstance(out_shapes, list)
    outs = [jax.ShapeDtypeStruct(s, F32) for s in (out_shapes if several else [out_shapes])]
    return pl.pallas_call(
        body,
        out_shape=outs if several else outs[0],
        scratch_shapes=list(scratch),
        cost_estimate=pl.CostEstimate(flops=flops, bytes_accessed=moved, transcendentals=0),
        compiler_params=pltpu.CompilerParams(vmem_limit_bytes=16 << 20),
    )


def lane_index(rows):
    return lax.broadcasted_iota(jnp.int32, (rows, LANES), 1)


def rolled(x, shift):
    shift %= LANES
    return x if shift == 0 else pltpu.roll(x, shift, 1)


def window(parts, start, rows):
    first, off = divmod(start, LANES)
    if off == 0:
        return parts(first)
    low, high = rolled(parts(first), -off), rolled(parts(first + 1), -off)
    return jnp.where(lane_index(rows) < LANES - off, low, high)


def pack_multiplier(m_ref, out_ref):
    groups = DEVICES // 4
    lane = lane_index(groups)
    for j in range(4):
        rest = None
        for i in range(PER):
            piece = lambda n, i=i: m_ref[pl.ds(4 * n + i, groups, stride=20), :]
            out_ref[pl.ds(5 * j + i, groups, stride=20), :] = window(piece, DEPTH * j, groups)
            tail = rolled(piece(j + 1), REST * (i - j))
            rest = tail if rest is None else jnp.where(lane >= REST * i, tail, rest)
        out_ref[pl.ds(5 * j + 4, groups, stride=20), :] = rest


def pack_swapped(m_ref, out_ref):
    groups = DEVICES // 4
    lane = lane_index(groups)
    for j in range(4):
        rest = None
        for i in range(PER):
            u = 4 * j + i
            main = None
            for c in range(PER):
                piece = lambda n, c=c: m_ref[pl.ds(4 * n + c, groups, stride=20), :]
                first, off = divmod(O * u, LANES)
                block = piece(first)
                if off + O > LANES:
                    block = jnp.where(lane >= off, block, piece(first + 1))
                at = O * c
                block_main = rolled(block, at - off)
                main = block_main if main is None else jnp.where(lane >= at, block_main, main)
                if at + O > LANES:
                    keep = LANES - at
                    tail = rolled(block, REST * i - off - keep)
                    rest = tail if rest is None else jnp.where(lane >= REST * i, tail, rest)
            out_ref[pl.ds(5 * j + i, groups, stride=20), :] = main
        out_ref[pl.ds(5 * j + 4, groups, stride=20), :] = rest


def pack_cycle(w_ref, out_ref):
    cols = w_ref.shape[0]
    count = w_ref.shape[1] // DEPTH
    lane = lane_index(8)
    for e in range(count):
        rest = None
        for g in range(cols // 8):
            piece = lambda n, g=g: w_ref[8 * g : 8 * g + 8, LANES * n : LANES * n + LANES]
            out_ref[40 * e + 8 * g : 40 * e + 8 * g + 8, :] = window(piece, DEPTH * e, 8)
            first, off = divmod(DEPTH * e + LANES, LANES)
            tail = rolled(piece(first), REST * g - off)
            rest = tail if rest is None else jnp.where(lane >= REST * g, tail, rest)
        out_ref[40 * e + 32 : 40 * e + 40, :] = rest


def update(got_ref, swapped_ref, w_ref, out_ref, x_ref, p_ref, pr_ref, q_ref, qr_ref):
    lane = lane_index(DEVICES)
    x_ref[...] = 2.0 * got_ref[...] - swapped_ref[...]
    packed = x_ref[pl.ds(4, DEVICES, stride=5), :]
    n_col = w_ref.shape[0] // 40
    n_row = DEVICES // n_col
    for i in range(PER):
        a_main = x_ref[pl.ds(i, DEVICES, stride=5), :]
        a_rest = rolled(packed, -REST * i)
        w_main = jnp.concatenate(
            [w_ref[pl.ds(4 * r + i, n_col, stride=40), :] for r in range(n_row)], axis=0
        )
        w_rest = jnp.concatenate(
            [
                rolled(w_ref[pl.ds(32 + 4 * (r % 2) + i, n_col, stride=40), :], REST * (1 - r // 2))
                for r in range(n_row)
            ],
            axis=0,
        )
        rows = slice(DEVICES * i, DEVICES * i + DEVICES)
        spread = pl.ds(i, DEVICES, stride=4)
        p_ref[rows, :LANES] = a_main
        p_ref[rows, LANES:] = w_main
        q_ref[0, spread, :] = w_main
        q_ref[1, spread, :] = a_main
        pr_ref[rows, :] = jnp.where(lane < REST, a_rest, jnp.where(lane < 2 * REST, w_rest, 0.0))
        w_first, a_second = rolled(w_rest, -REST), rolled(a_rest, REST)
        qr_ref[spread, :] = jnp.where(lane < REST, w_first, jnp.where(lane < 2 * REST, a_second, 0.0))

    def product(x, y):
        return lax.dot_general(
            x, y, (((1,), (1,)), ((), ())), precision=lax.Precision.HIGHEST, preferred_element_type=F32
        )

    for i in range(PER):
        rows = slice(DEVICES * i, DEVICES * i + DEVICES)
        term = product(p_ref[rows, :LANES], q_ref[0])
        term += product(p_ref[rows, LANES:], q_ref[1])
        term += product(pr_ref[rows, :], qr_ref[...])
        for m in range(V // LANES):
            out_ref[pl.ds(4 * m + i, DEVICES, stride=ROWS_OUT), :] = term[:, LANES * m : LANES * m + LANES]


def finish(parts_ref, out_ref):
    total = parts_ref[0:ROWS_OUT, :]
    for n in range(1, parts_ref.shape[0] // ROWS_OUT):
        total += parts_ref[ROWS_OUT * n : ROWS_OUT * n + ROWS_OUT, :]
    for m in range(V // LANES):
        out_ref[:, LANES * m : LANES * m + LANES] = total[4 * m : 4 * m + 4, :]


def on_device(multiplier, cycle_tiles):
    n_col = lax.axis_size("col")
    both = ("row", "col")
    slab = multiplier.reshape(PER, DEPTH, LANES).transpose(1, 0, 2).reshape(PER * DEPTH, LANES)
    cycle_rows = cycle_tiles.T
    packed = call(pack_multiplier, (5 * DEVICES, LANES))(slab)
    got = lax.all_to_all(packed.reshape(DEVICES, 1, 5 * LANES), both, 0, 0, tiled=True)
    w_packed = call(pack_cycle, (40 * n_col, LANES))(cycle_rows)
    w_got = lax.all_to_all(w_packed.reshape(n_col, 40, LANES), "col", 0, 0, tiled=True)
    swapped = call(pack_swapped, (5 * DEVICES, LANES))(slab)
    share = call(
        update,
        (ROWS_OUT * DEVICES, LANES),
        scratch=[
            VMEM((5 * DEVICES, LANES), F32),
            VMEM((V, 2 * LANES), F32),
            VMEM((V, LANES), F32),
            VMEM((2, V, LANES), F32),
            VMEM((V, LANES), F32),
        ],
        flops=2 * V * V * 2 * DEPTH * 6,
    )(got.reshape(5 * DEVICES, LANES), swapped, w_got.reshape(40 * n_col, LANES))
    parts = lax.all_to_all(share.reshape(DEVICES, ROWS_OUT, LANES), both, 0, 0, tiled=True)
    return call(finish, (PER, V))(parts.reshape(DEVICES * ROWS_OUT, LANES))


def solution(mesh):
    placed = (P(("row", "col"), None), P("row", "col"))
    return jax.shard_map(
        on_device, mesh=mesh, in_specs=placed, out_specs=P(("row", "col"), None), check_vma=False
    )
```

```python
import jax
import jax.numpy as jnp
from jax import lax
from jax.experimental import pallas as pl
from jax.experimental.pallas import tpu as pltpu
from jax.sharding import Mesh, PartitionSpec as P

O = 40
V = 512
LANES = 128
PER = 4
DEPTH = PER * O
REST = DEPTH - LANES
DEVICES = V // PER
CHIPS = DEVICES // 2
ROWS_OUT = PER * V // LANES
CHUNK = 40
N_YZ = 8
FAR = (0, 4)

VMEM = pltpu.VMEM
F32 = jnp.float32


def call(body, out_shapes, scratch=(), flops=0, moved=1 << 20):
    several = isinstance(out_shapes, list)
    outs = [jax.ShapeDtypeStruct(s, F32) for s in (out_shapes if several else [out_shapes])]
    return pl.pallas_call(
        body,
        out_shape=outs if several else outs[0],
        scratch_shapes=list(scratch),
        cost_estimate=pl.CostEstimate(flops=flops, bytes_accessed=moved, transcendentals=0),
        compiler_params=pltpu.CompilerParams(vmem_limit_bytes=16 << 20),
    )


def lane_index(rows):
    return lax.broadcasted_iota(jnp.int32, (rows, LANES), 1)


def rolled(x, shift):
    shift %= LANES
    return x if shift == 0 else pltpu.roll(x, shift, 1)


def window(parts, start, rows):
    first, off = divmod(start, LANES)
    if off == 0:
        return parts(first)
    low, high = rolled(parts(first), -off), rolled(parts(first + 1), -off)
    return jnp.where(lane_index(rows) < LANES - off, low, high)


def chunk(n):
    return pl.ds(CHUNK * n if isinstance(n, int) else pl.multiple_of(CHUNK * n, 8), CHUNK)


def pack_multiplier(m_ref, out_ref):
    groups = DEVICES // 4
    lane = lane_index(groups)
    for j in range(4):
        rest = None
        for i in range(PER):
            piece = lambda n, i=i: m_ref[pl.ds(4 * n + i, groups, stride=20), :]
            out_ref[pl.ds(5 * j + i, groups, stride=20), :] = window(piece, DEPTH * j, groups)
            tail = rolled(piece(j + 1), REST * (i - j))
            rest = tail if rest is None else jnp.where(lane >= REST * i, tail, rest)
        out_ref[pl.ds(5 * j + 4, groups, stride=20), :] = rest


def pack_swapped(m_ref, out_ref):
    groups = DEVICES // 4
    lane = lane_index(groups)
    for j in range(4):
        rest = None
        for i in range(PER):
            u = 4 * j + i
            main = None
            for c in range(PER):
                piece = lambda n, c=c: m_ref[pl.ds(4 * n + c, groups, stride=20), :]
                first, off = divmod(O * u, LANES)
                block = piece(first)
                if off + O > LANES:
                    block = jnp.where(lane >= off, block, piece(first + 1))
                at = O * c
                block_main = rolled(block, at - off)
                main = block_main if main is None else jnp.where(lane >= at, block_main, main)
                if at + O > LANES:
                    keep = LANES - at
                    tail = rolled(block, REST * i - off - keep)
                    rest = tail if rest is None else jnp.where(lane >= REST * i, tail, rest)
            out_ref[pl.ds(5 * j + i, groups, stride=20), :] = main
        out_ref[pl.ds(5 * j + 4, groups, stride=20), :] = rest


def pack_cycle(w_ref, own_ref, other_ref, all_ref):
    lane = lane_index(8)
    for e in range(2 * N_YZ):
        rest = None
        for g in range(PER):
            piece = lambda n, g=g: w_ref[8 * g : 8 * g + 8, LANES * n : LANES * n + LANES]
            all_ref[CHUNK * e + 8 * g : CHUNK * e + 8 * g + 8, :] = window(piece, DEPTH * e, 8)
            first, off = divmod(DEPTH * e + LANES, LANES)
            tail = rolled(piece(first), REST * g - off)
            rest = tail if rest is None else jnp.where(lane >= REST * g, tail, rest)
        all_ref[CHUNK * e + 32 : CHUNK * e + 40, :] = rest
    core = lax.axis_index("core")
    for yz in range(N_YZ):
        own_ref[chunk(yz), :] = all_ref[chunk(2 * yz + core), :]
        other_ref[chunk(yz), :] = all_ref[chunk(2 * yz + 1 - core), :]


def turn_far(own_ref, other_ref, *out_refs):
    me = lax.axis_index("yz")
    for k, ref in zip(FAR, out_refs):
        for z in range(4):
            for s, came in enumerate((own_ref, other_ref)):
                ref[chunk(2 * z + s), :] = came[chunk(((me ^ k) & 4) + z), :]


def turn_near(*refs):
    came, out_refs = refs[: len(FAR)], refs[len(FAR) :]
    z = lax.axis_index("yz") & 3
    for j, ref in enumerate(out_refs):
        for n, piece in enumerate(came):
            for s in range(2):
                ref[chunk(2 * n + s), :] = piece[chunk(2 * (z ^ j) + s), :]


def product(x, y):
    return lax.dot_general(
        x, y, (((1,), (1,)), ((), ())), precision=lax.Precision.HIGHEST, preferred_element_type=F32
    )


def half_update(p_ref, q_ref, out_ref):
    term = product(p_ref[...], jnp.concatenate([q_ref[n] for n in range(3)], axis=1))
    for i in range(PER):
        for m in range(V // LANES):
            piece = term[CHIPS * i : CHIPS * i + CHIPS, LANES * m : LANES * m + LANES]
            out_ref[pl.ds(4 * m + i, CHIPS, stride=ROWS_OUT), :] = piece


def first_half(got_ref, swapped_ref, w0, w1, w2, w3, out_ref, p_own, q_ref, x_ref, w_ref, p_ref):
    me, core = lax.axis_index("yz"), lax.axis_index("core")
    for j, ref in enumerate((w0, w1, w2, w3)):
        for n, k in enumerate(FAR):
            for s in range(2):
                w_ref[chunk(2 * (me ^ k ^ j) + (core ^ s)), :] = ref[chunk(2 * n + s), :]
    x_ref[...] = 2.0 * got_ref[...] - swapped_ref[...]
    lane = lane_index(CHIPS)
    n_row = DEVICES // (2 * N_YZ)
    for parity, p_out in ((1 - core, p_ref), (core, p_own)):
        packed = x_ref[pl.ds(5 * parity + 4, CHIPS, stride=10), :]
        for i in range(PER):
            a_main = x_ref[pl.ds(5 * parity + i, CHIPS, stride=10), :]
            a_rest = rolled(packed, -REST * i)
            w_main = jnp.concatenate(
                [w_ref[pl.ds(CHUNK * parity + 4 * r + i, N_YZ, stride=2 * CHUNK), :] for r in range(n_row)], axis=0
            )
            w_rest = jnp.concatenate(
                [
                    rolled(
                        w_ref[pl.ds(CHUNK * parity + 32 + 4 * (r % 2) + i, N_YZ, stride=2 * CHUNK), :],
                        REST * (1 - r // 2),
                    )
                    for r in range(n_row)
                ],
                axis=0,
            )
            rows = slice(CHIPS * i, CHIPS * i + CHIPS)
            spread = pl.ds(4 * parity + i, CHIPS, stride=8)
            p_out[rows, :LANES] = a_main
            p_out[rows, LANES : 2 * LANES] = w_main
            q_ref[0, spread, :] = w_main
            q_ref[1, spread, :] = a_main
            p_out[rows, 2 * LANES :] = jnp.where(lane < REST, a_rest, jnp.where(lane < 2 * REST, w_rest, 0.0))
            w_first, a_second = rolled(w_rest, -REST), rolled(a_rest, REST)
            q_ref[2, spread, :] = jnp.where(
                lane < REST, w_first, jnp.where(lane < 2 * REST, a_second, 0.0)
            )
    half_update(p_ref, q_ref, out_ref)


def finish(parts_ref, out_ref):
    total = parts_ref[0:ROWS_OUT, :]
    for n in range(1, parts_ref.shape[0] // ROWS_OUT):
        total += parts_ref[ROWS_OUT * n : ROWS_OUT * n + ROWS_OUT, :]
    for m in range(V // LANES):
        out_ref[:, LANES * m : LANES * m + LANES] = total[4 * m : 4 * m + 4, :]


def swap(x, axis, k):
    return lax.ppermute(x, axis, [(n, n ^ k) for n in range(lax.axis_size(axis))])


def on_device(multiplier, cycle_tiles):
    slab = multiplier.reshape(PER, DEPTH, LANES).transpose(1, 0, 2).reshape(PER * DEPTH, LANES)
    half, quarter = (N_YZ * CHUNK, LANES), (4 * CHUNK, LANES)
    own, other = call(pack_cycle, [half] * 2, scratch=[VMEM((2 * N_YZ * CHUNK, LANES), F32)])(cycle_tiles.T)
    other = swap(other, "core", 1)
    packed = call(pack_multiplier, (5 * DEVICES, LANES))(slab)
    far = call(turn_far, [half] * 2)(own, other)
    far = [far[0], *(swap(x, "yz", k) for k, x in zip(FAR[1:], far[1:]))]
    got = lax.all_to_all(
        packed.reshape(DEVICES, 1, 5 * LANES), ("row", "yz", "core"), 0, 0, tiled=True
    )
    near = call(turn_near, [quarter] * 4)(*far)
    near = [near[0], *(swap(x, "yz", j) for j, x in enumerate(near) if j)]
    swapped = call(pack_swapped, (5 * DEVICES, LANES))(slab)
    width = 3 * LANES
    rows, flops = CHIPS * ROWS_OUT, V * V * width * 6
    theirs, p_own, q = call(
        first_half,
        [(rows, LANES), (V // 2, width), (3, V, LANES)],
        scratch=[
            VMEM((5 * DEVICES, LANES), F32),
            VMEM((2 * N_YZ * CHUNK, LANES), F32),
            VMEM((V // 2, width), F32),
        ],
        flops=flops,
    )(got.reshape(5 * DEVICES, LANES), swapped, *near)
    theirs = swap(theirs, "core", 1)
    mine = call(half_update, (rows, LANES), flops=flops)(p_own, q)
    share = mine + theirs
    parts = lax.all_to_all(share.reshape(CHIPS, ROWS_OUT, LANES), ("row", "yz"), 0, 0, tiled=True)
    return call(finish, (PER, V))(parts.reshape(rows, LANES))


def solution(mesh):
    n_row = mesh.shape["row"]
    split = Mesh(mesh.devices.reshape(n_row, N_YZ, 2), ("row", "yz", "core"))
    every = ("row", "yz", "core")
    return jax.shard_map(
        on_device,
        mesh=split,
        in_specs=(P(every, None), P("row", ("yz", "core"))),
        out_specs=P(every, None),
        check_vma=False,
    )
```

```python
import jax
import jax.numpy as jnp
from jax import lax
from jax.experimental import pallas as pl
from jax.experimental.pallas import tpu as pltpu
from jax.sharding import Mesh, PartitionSpec as P

O = 40
V = 512
LANES = 128
PER = 4
DEPTH = PER * O
REST = DEPTH - LANES
DEVICES = V // PER
CHIPS = DEVICES // 2
ROWS_OUT = PER * V // LANES
CHUNK = 40
N_YZ = 8
FAR = (0, 4)

VMEM = pltpu.VMEM
F32 = jnp.float32


def call(body, out_shapes, scratch=(), flops=0, moved=1 << 20, **specs):
    several = isinstance(out_shapes, list)
    outs = [
        s if isinstance(s, jax.ShapeDtypeStruct) else jax.ShapeDtypeStruct(s, F32)
        for s in (out_shapes if several else [out_shapes])
    ]
    return pl.pallas_call(
        body,
        out_shape=outs if several else outs[0],
        scratch_shapes=list(scratch),
        **specs,
        cost_estimate=pl.CostEstimate(flops=flops, bytes_accessed=moved, transcendentals=0),
        compiler_params=pltpu.CompilerParams(vmem_limit_bytes=16 << 20),
    )


def lane_index(rows):
    return lax.broadcasted_iota(jnp.int32, (rows, LANES), 1)


def rolled(x, shift):
    shift %= LANES
    return x if shift == 0 else pltpu.roll(x, shift, 1)


def window(parts, start, rows):
    first, off = divmod(start, LANES)
    if off == 0:
        return parts(first)
    low, high = rolled(parts(first), -off), rolled(parts(first + 1), -off)
    return jnp.where(lane_index(rows) < LANES - off, low, high)


def chunk(n):
    return pl.ds(CHUNK * n if isinstance(n, int) else pl.multiple_of(CHUNK * n, 8), CHUNK)


def pack_multiplier(m_ref, out_ref):
    groups = DEVICES // 4
    lane = lane_index(groups)
    for j in range(4):
        rest = None
        for i in range(PER):
            piece = lambda n, i=i: m_ref[pl.ds(4 * n + i, groups, stride=20), :]
            out_ref[pl.ds(5 * j + i, groups, stride=20), :] = window(piece, DEPTH * j, groups)
            tail = rolled(piece(j + 1), REST * (i - j))
            rest = tail if rest is None else jnp.where(lane >= REST * i, tail, rest)
        out_ref[pl.ds(5 * j + 4, groups, stride=20), :] = rest


def pack_swapped(m_ref, out_ref):
    groups = DEVICES // 4
    lane = lane_index(groups)
    for j in range(4):
        rest = None
        for i in range(PER):
            u = 4 * j + i
            main = None
            for c in range(PER):
                piece = lambda n, c=c: m_ref[pl.ds(4 * n + c, groups, stride=20), :]
                first, off = divmod(O * u, LANES)
                block = piece(first)
                if off + O > LANES:
                    block = jnp.where(lane >= off, block, piece(first + 1))
                at = O * c
                block_main = rolled(block, at - off)
                main = block_main if main is None else jnp.where(lane >= at, block_main, main)
                if at + O > LANES:
                    keep = LANES - at
                    tail = rolled(block, REST * i - off - keep)
                    rest = tail if rest is None else jnp.where(lane >= REST * i, tail, rest)
            out_ref[pl.ds(5 * j + i, groups, stride=20), :] = main
        out_ref[pl.ds(5 * j + 4, groups, stride=20), :] = rest


def pack_cycle(w_hbm, m_hbm, own_ref, other_ref, m_ref, w_ref, all_ref, sems):
    w_copy = pltpu.make_async_copy(w_hbm, w_ref, sems.at[0])
    m_copy = pltpu.make_async_copy(m_hbm, m_ref, sems.at[1])
    w_copy.start()
    m_copy.start()
    w_copy.wait()
    lane = lane_index(8)
    for e in range(2 * N_YZ):
        rest = None
        for g in range(PER):
            piece = lambda n, g=g: w_ref[8 * g : 8 * g + 8, LANES * n : LANES * n + LANES]
            all_ref[CHUNK * e + 8 * g : CHUNK * e + 8 * g + 8, :] = window(piece, DEPTH * e, 8)
            first, off = divmod(DEPTH * e + LANES, LANES)
            tail = rolled(piece(first), REST * g - off)
            rest = tail if rest is None else jnp.where(lane >= REST * g, tail, rest)
        all_ref[CHUNK * e + 32 : CHUNK * e + 40, :] = rest
    core = lax.axis_index("core")
    for yz in range(N_YZ):
        own_ref[chunk(yz), :] = all_ref[chunk(2 * yz + core), :]
        other_ref[chunk(yz), :] = all_ref[chunk(2 * yz + 1 - core), :]
    m_copy.wait()


def turn_far(own_ref, other_ref, *out_refs):
    me = lax.axis_index("yz")
    for k, ref in zip(FAR, out_refs):
        for z in range(4):
            for s, came in enumerate((own_ref, other_ref)):
                ref[chunk(2 * z + s), :] = came[chunk(((me ^ k) & 4) + z), :]


def turn_near(*refs):
    came, out_refs = refs[: len(FAR)], refs[len(FAR) :]
    z = lax.axis_index("yz") & 3
    for j, ref in enumerate(out_refs):
        for n, piece in enumerate(came):
            for s in range(2):
                ref[chunk(2 * n + s), :] = piece[chunk(2 * (z ^ j) + s), :]


def split(x):
    high = x.astype(jnp.bfloat16)
    return high, (x - high.astype(F32)).astype(jnp.bfloat16)


def left_side(parts):
    high, low = split(jnp.concatenate(parts, axis=1))
    return jnp.concatenate([high, high, low], axis=1)


def right_side(parts):
    high, low = split(jnp.concatenate(parts, axis=1))
    return jnp.concatenate([high, low, high], axis=1)


def half_update(p_ref, q_ref, out_ref):
    term = lax.dot_general(
        p_ref[...], q_ref[...], (((1,), (1,)), ((), ())), preferred_element_type=F32
    )
    for i in range(PER):
        for m in range(V // LANES):
            piece = term[CHIPS * i : CHIPS * i + CHIPS, LANES * m : LANES * m + LANES]
            out_ref[pl.ds(4 * m + i, CHIPS, stride=ROWS_OUT), :] = piece


def arrange_slab(got_ref, swapped_ref, by_core_ref, by_row_ref, x_ref):
    core = lax.axis_index("core")
    x_ref[...] = 2.0 * got_ref[...] - swapped_ref[...]
    for h, parity in enumerate((1 - core, core)):
        packed = x_ref[pl.ds(5 * parity + 4, CHIPS, stride=10), :]
        for i in range(PER):
            parts = x_ref[pl.ds(5 * parity + i, CHIPS, stride=10), :], rolled(packed, -REST * i)
            for n, part in enumerate(parts):
                by_core_ref[n, h, CHIPS * i : CHIPS * i + CHIPS, :] = part
                by_row_ref[n, pl.ds(4 * parity + i, CHIPS, stride=8), :] = part


def first_half(a_core, a_row, w0, w1, w2, w3, out_ref, p_own, q_ref, w_ref, w_core, w_row, p_ref):
    me, core = lax.axis_index("yz"), lax.axis_index("core")
    for j, ref in enumerate((w0, w1, w2, w3)):
        for n, k in enumerate(FAR):
            for s in range(2):
                w_ref[chunk(2 * (me ^ k ^ j) + (core ^ s)), :] = ref[chunk(2 * n + s), :]
    n_row = DEVICES // (2 * N_YZ)
    for h, parity in enumerate((1 - core, core)):
        for i in range(PER):
            for r in range(n_row):
                first = CHUNK * parity + 4 * r + i, CHUNK * parity + 32 + 4 * (r % 2) + i
                for n, at in enumerate(first):
                    part = w_ref[pl.ds(at, N_YZ, stride=2 * CHUNK), :]
                    part = rolled(part, -REST * (r // 2)) if n else part
                    begin = CHIPS * i + N_YZ * r
                    w_core[n, h, begin : begin + N_YZ, :] = part
                    w_row[n, pl.ds(8 * N_YZ * r + 4 * parity + i, N_YZ, stride=8), :] = part

    def both(x, y):
        lane = lane_index(x.shape[0])
        return jnp.where(lane < REST, x, jnp.where(lane < 2 * REST, rolled(y, REST), 0.0))

    q_ref[...] = right_side([w_row[0], a_row[0], both(w_row[1], a_row[1])])
    for h, ref in enumerate((p_ref, p_own)):
        ref[...] = left_side([a_core[0, h], w_core[0, h], both(a_core[1, h], w_core[1, h])])
    half_update(p_ref, q_ref, out_ref)


def finish(parts_ref, out_ref):
    total = parts_ref[0:ROWS_OUT, :]
    for n in range(1, parts_ref.shape[0] // ROWS_OUT):
        total += parts_ref[ROWS_OUT * n : ROWS_OUT * n + ROWS_OUT, :]
    for m in range(V // LANES):
        out_ref[:, LANES * m : LANES * m + LANES] = total[4 * m : 4 * m + 4, :]


def swap(x, axis, k):
    return lax.ppermute(x, axis, [(n, n ^ k) for n in range(lax.axis_size(axis))])


def on_device(multiplier, cycle_tiles):
    slab = multiplier.reshape(PER, DEPTH, LANES).transpose(1, 0, 2).reshape(PER * DEPTH, LANES)
    half, quarter = (N_YZ * CHUNK, LANES), (4 * CHUNK, LANES)
    columns = cycle_tiles.T
    own, other, slab = call(
        pack_cycle,
        [half, half, slab.shape],
        scratch=[
            VMEM(columns.shape, F32),
            VMEM((2 * N_YZ * CHUNK, LANES), F32),
            pltpu.SemaphoreType.DMA((2,)),
        ],
        in_specs=[pl.BlockSpec(memory_space=pltpu.HBM)] * 2,
        out_specs=[pl.BlockSpec(memory_space=VMEM)] * 3,
    )(*(pltpu.with_memory_space_constraint(x, pltpu.HBM) for x in (columns, slab)))
    other = swap(other, "core", 1)
    packed = call(pack_multiplier, (5 * DEVICES, LANES))(slab)
    far = call(turn_far, [half] * 2)(own, other)
    far = [far[0], *(swap(x, "yz", k) for k, x in zip(FAR[1:], far[1:]))]
    got = lax.all_to_all(
        packed.reshape(DEVICES, 1, 5 * LANES), ("row", "yz", "core"), 0, 0, tiled=True
    )
    near = call(turn_near, [quarter] * 4)(*far)
    near = [near[0], *(swap(x, "yz", j) for j, x in enumerate(near) if j)]
    swapped = call(pack_swapped, (5 * DEVICES, LANES))(slab)
    width = 9 * LANES
    rows, flops = CHIPS * ROWS_OUT, V * V * width
    by_core, by_row = (2, 2, V // 2, LANES), (2, V, LANES)
    a_core, a_row = call(arrange_slab, [by_core, by_row], scratch=[VMEM((5 * DEVICES, LANES), F32)])(
        got.reshape(5 * DEVICES, LANES), swapped
    )
    sides = [jax.ShapeDtypeStruct((n, width), jnp.bfloat16) for n in (V // 2, V)]
    theirs, p_own, q = call(
        first_half,
        [(rows, LANES), *sides],
        scratch=[
            VMEM((2 * N_YZ * CHUNK, LANES), F32),
            VMEM(by_core, F32),
            VMEM(by_row, F32),
            VMEM((V // 2, width), jnp.bfloat16),
        ],
        flops=flops,
    )(a_core, a_row, *near)
    theirs = swap(theirs, "core", 1)
    mine = call(half_update, (rows, LANES), flops=flops)(p_own, q)
    share = mine + theirs
    parts = lax.all_to_all(share.reshape(CHIPS, ROWS_OUT, LANES), ("row", "yz"), 0, 0, tiled=True)
    return call(finish, (PER, V))(parts.reshape(rows, LANES))


def solution(mesh):
    n_row = mesh.shape["row"]
    split = Mesh(mesh.devices.reshape(n_row, N_YZ, 2), ("row", "yz", "core"))
    every = ("row", "yz", "core")
    return jax.shard_map(
        on_device,
        mesh=split,
        in_specs=(P(every, None), P("row", ("yz", "core"))),
        out_specs=P(every, None),
        check_vma=False,
    )
```

```python
import jax
import jax.numpy as jnp
from jax import lax
from jax.experimental import pallas as pl
from jax.experimental.pallas import tpu as pltpu
from jax.sharding import Mesh, PartitionSpec as P

O = 40
V = 512
LANES = 128
PER = 4
DEPTH = PER * O
REST = DEPTH - LANES
DEVICES = V // PER
CHIPS = DEVICES // 2
ROWS_OUT = PER * V // LANES
CHUNK = 40
N_YZ = 8
FAR = (0, 4)

VMEM = pltpu.VMEM
F32 = jnp.float32


def call(body, out_shapes, scratch=(), flops=0, moved=1 << 20, **specs):
    several = isinstance(out_shapes, list)
    outs = [
        s if isinstance(s, jax.ShapeDtypeStruct) else jax.ShapeDtypeStruct(s, F32)
        for s in (out_shapes if several else [out_shapes])
    ]
    return pl.pallas_call(
        body,
        out_shape=outs if several else outs[0],
        scratch_shapes=list(scratch),
        **specs,
        cost_estimate=pl.CostEstimate(flops=flops, bytes_accessed=moved, transcendentals=0),
        compiler_params=pltpu.CompilerParams(vmem_limit_bytes=16 << 20),
    )


def lane_index(rows):
    return lax.broadcasted_iota(jnp.int32, (rows, LANES), 1)


def rolled(x, shift):
    shift %= LANES
    return x if shift == 0 else pltpu.roll(x, shift, 1)


def window(parts, start, rows):
    first, off = divmod(start, LANES)
    if off == 0:
        return parts(first)
    low, high = rolled(parts(first), -off), rolled(parts(first + 1), -off)
    return jnp.where(lane_index(rows) < LANES - off, low, high)


def chunk(n):
    return pl.ds(CHUNK * n if isinstance(n, int) else pl.multiple_of(CHUNK * n, 8), CHUNK)


def pack_multiplier(m_ref, out_ref):
    groups = DEVICES // 4
    lane = lane_index(groups)
    for j in range(4):
        rest = None
        for i in range(PER):
            piece = lambda n, i=i: m_ref[pl.ds(4 * n + i, groups, stride=20), :]
            out_ref[pl.ds(5 * j + i, groups, stride=20), :] = window(piece, DEPTH * j, groups)
            tail = rolled(piece(j + 1), REST * (i - j))
            rest = tail if rest is None else jnp.where(lane >= REST * i, tail, rest)
        out_ref[pl.ds(5 * j + 4, groups, stride=20), :] = rest


def pack_swapped(m_ref, out_ref):
    groups = DEVICES // 4
    lane = lane_index(groups)
    for j in range(4):
        rest = None
        for i in range(PER):
            u = 4 * j + i
            main = None
            for c in range(PER):
                piece = lambda n, c=c: m_ref[pl.ds(4 * n + c, groups, stride=20), :]
                first, off = divmod(O * u, LANES)
                block = piece(first)
                if off + O > LANES:
                    block = jnp.where(lane >= off, block, piece(first + 1))
                at = O * c
                block_main = rolled(block, at - off)
                main = block_main if main is None else jnp.where(lane >= at, block_main, main)
                if at + O > LANES:
                    keep = LANES - at
                    tail = rolled(block, REST * i - off - keep)
                    rest = tail if rest is None else jnp.where(lane >= REST * i, tail, rest)
            out_ref[pl.ds(5 * j + i, groups, stride=20), :] = main
        out_ref[pl.ds(5 * j + 4, groups, stride=20), :] = rest


def pack_cycle(w_hbm, m_hbm, own_ref, other_ref, m_ref, w_ref, all_ref, sems):
    w_copy = pltpu.make_async_copy(w_hbm, w_ref, sems.at[0])
    m_copy = pltpu.make_async_copy(m_hbm, m_ref, sems.at[1])
    w_copy.start()
    m_copy.start()
    w_copy.wait()
    rest = [None] * (2 * N_YZ)
    lane = lane_index(8)
    for g in range(PER):
        for e in range(2 * N_YZ):
            piece = lambda n, g=g: w_ref[8 * g : 8 * g + 8, LANES * n : LANES * n + LANES]
            all_ref[CHUNK * e + 8 * g : CHUNK * e + 8 * g + 8, :] = window(piece, DEPTH * e, 8)
            first, off = divmod(DEPTH * e + LANES, LANES)
            tail = rolled(piece(first), REST * g - off)
            rest[e] = tail if g == 0 else jnp.where(lane >= REST * g, tail, rest[e])
    for e in range(2 * N_YZ):
        all_ref[CHUNK * e + 32 : CHUNK * e + 40, :] = rest[e]
    core = lax.axis_index("core")
    for yz in range(N_YZ):
        own_ref[chunk(yz), :] = all_ref[chunk(2 * yz + core), :]
        other_ref[chunk(yz), :] = all_ref[chunk(2 * yz + 1 - core), :]
    m_copy.wait()


def turn_far(own_ref, other_ref, *out_refs):
    me = lax.axis_index("yz")
    for k, ref in zip(FAR, out_refs):
        for z in range(4):
            for s, came in enumerate((own_ref, other_ref)):
                ref[chunk(2 * z + s), :] = came[chunk(((me ^ k) & 4) + z), :]


def turn_near(*refs):
    came, out_refs = refs[: len(FAR)], refs[len(FAR) :]
    z = lax.axis_index("yz") & 3
    for j, ref in enumerate(out_refs):
        for n, piece in enumerate(came):
            for s in range(2):
                ref[chunk(2 * n + s), :] = piece[chunk(2 * (z ^ j) + s), :]


def split(x):
    high = x.astype(jnp.bfloat16)
    return high, (x - high.astype(F32)).astype(jnp.bfloat16)


def rest_side(x, y, swapped):
    lane = lane_index(x.shape[0])
    both = jnp.where(lane < REST, x, rolled(y, REST))
    high, low = split(jnp.where(lane < 2 * REST, both, 0.0))
    wide = high.astype(F32), low.astype(F32)
    first, second = (wide[0], wide[0]) if swapped else wide
    third = low if swapped else high
    return [(first + rolled(second, LANES // 2)).astype(jnp.bfloat16), third]


def left_side(slab, cycle, slab_rest, cycle_rest):
    (a, a_low), (w, w_low) = split(slab), split(cycle)
    return jnp.concatenate([a, a_low, w, w_low, a, w, *rest_side(slab_rest, cycle_rest, False)], axis=1)


def right_side(cycle, slab, cycle_rest, slab_rest):
    (w, w_low), (a, a_low) = split(cycle), split(slab)
    return jnp.concatenate([w, w, a, a, w_low, a_low, *rest_side(cycle_rest, slab_rest, True)], axis=1)


def half_update(p_ref, q_ref, out_ref):
    term = lax.dot_general(
        p_ref[...], q_ref[...], (((1,), (1,)), ((), ())), preferred_element_type=F32
    )
    for i in range(PER):
        for m in range(V // LANES):
            piece = term[CHIPS * i : CHIPS * i + CHIPS, LANES * m : LANES * m + LANES]
            out_ref[pl.ds(4 * m + i, CHIPS, stride=ROWS_OUT), :] = piece


def arrange_slab(got_ref, swapped_ref, by_core_ref, by_row_ref, x_ref):
    core = lax.axis_index("core")
    x_ref[...] = 2.0 * got_ref[...] - swapped_ref[...]
    for h, parity in enumerate((1 - core, core)):
        packed = x_ref[pl.ds(5 * parity + 4, CHIPS, stride=10), :]
        for i in range(PER):
            parts = x_ref[pl.ds(5 * parity + i, CHIPS, stride=10), :], rolled(packed, -REST * i)
            for n, part in enumerate(parts):
                by_core_ref[n, h, CHIPS * i : CHIPS * i + CHIPS, :] = part
                by_row_ref[n, pl.ds(4 * parity + i, CHIPS, stride=8), :] = part


def first_half(a_core, a_row, w0, w1, w2, w3, out_ref, w_core, q_ref, w_ref, w_row, p_ref):
    me, core = lax.axis_index("yz"), lax.axis_index("core")
    for j, ref in enumerate((w0, w1, w2, w3)):
        for n, k in enumerate(FAR):
            for s in range(2):
                w_ref[chunk(2 * (me ^ k ^ j) + (core ^ s)), :] = ref[chunk(2 * n + s), :]
    n_row = DEVICES // (2 * N_YZ)
    for h, parity in enumerate((1 - core, core)):
        for i in range(PER):
            for r in range(n_row):
                first = CHUNK * parity + 4 * r + i, CHUNK * parity + 32 + 4 * (r % 2) + i
                for n, at in enumerate(first):
                    part = w_ref[pl.ds(at, N_YZ, stride=2 * CHUNK), :]
                    part = rolled(part, -REST * (r // 2)) if n else part
                    begin = CHIPS * i + N_YZ * r
                    w_core[n, h, begin : begin + N_YZ, :] = part
                    w_row[n, pl.ds(8 * N_YZ * r + 4 * parity + i, N_YZ, stride=8), :] = part

    q_ref[...] = right_side(w_row[0], a_row[0], w_row[1], a_row[1])
    p_ref[...] = left_side(a_core[0, 0], w_core[0, 0], a_core[1, 0], w_core[1, 0])
    half_update(p_ref, q_ref, out_ref)


def second_half(a_core, w_core, q_ref, out_ref, p_ref):
    p_ref[...] = left_side(a_core[0, 1], w_core[0, 1], a_core[1, 1], w_core[1, 1])
    half_update(p_ref, q_ref, out_ref)


def finish(parts_ref, out_ref):
    total = parts_ref[0:ROWS_OUT, :]
    for n in range(1, parts_ref.shape[0] // ROWS_OUT):
        total += parts_ref[ROWS_OUT * n : ROWS_OUT * n + ROWS_OUT, :]
    for m in range(V // LANES):
        out_ref[:, LANES * m : LANES * m + LANES] = total[4 * m : 4 * m + 4, :]


def swap(x, axis, k):
    return lax.ppermute(x, axis, [(n, n ^ k) for n in range(lax.axis_size(axis))])


def on_device(multiplier, cycle_tiles):
    slab = multiplier.reshape(PER, DEPTH, LANES).transpose(1, 0, 2).reshape(PER * DEPTH, LANES)
    half, quarter = (N_YZ * CHUNK, LANES), (4 * CHUNK, LANES)
    columns = cycle_tiles.T
    own, other, slab = call(
        pack_cycle,
        [half, half, slab.shape],
        scratch=[
            VMEM(columns.shape, F32),
            VMEM((2 * N_YZ * CHUNK, LANES), F32),
            pltpu.SemaphoreType.DMA((2,)),
        ],
        in_specs=[pl.BlockSpec(memory_space=pltpu.HBM)] * 2,
        out_specs=[pl.BlockSpec(memory_space=VMEM)] * 3,
    )(*(pltpu.with_memory_space_constraint(x, pltpu.HBM) for x in (columns, slab)))
    other = swap(other, "core", 1)
    packed = call(pack_multiplier, (5 * DEVICES, LANES))(slab)
    far = call(turn_far, [half] * 2)(own, other)
    far = [far[0], *(swap(x, "yz", k) for k, x in zip(FAR[1:], far[1:]))]
    got = lax.all_to_all(
        packed.reshape(DEVICES, 1, 5 * LANES), ("row", "yz", "core"), 0, 0, tiled=True
    )
    near = call(turn_near, [quarter] * 4)(*far)
    near = [near[0], *(swap(x, "yz", j) for j, x in enumerate(near) if j)]
    swapped = call(pack_swapped, (5 * DEVICES, LANES))(slab)
    width = 8 * LANES
    rows, flops = CHIPS * ROWS_OUT, V * V * width
    by_core, by_row = (2, 2, V // 2, LANES), (2, V, LANES)
    a_core, a_row = call(arrange_slab, [by_core, by_row], scratch=[VMEM((5 * DEVICES, LANES), F32)])(
        got.reshape(5 * DEVICES, LANES), swapped
    )
    left = VMEM((V // 2, width), jnp.bfloat16)
    theirs, w_core, q = call(
        first_half,
        [(rows, LANES), by_core, jax.ShapeDtypeStruct((V, width), jnp.bfloat16)],
        scratch=[VMEM((2 * N_YZ * CHUNK, LANES), F32), VMEM(by_row, F32), left],
        flops=flops,
    )(a_core, a_row, *near)
    theirs = swap(theirs, "core", 1)
    mine = call(second_half, (rows, LANES), scratch=[left], flops=flops)(a_core, w_core, q)
    share = mine + theirs
    parts = lax.all_to_all(share.reshape(CHIPS, ROWS_OUT, LANES), ("row", "yz"), 0, 0, tiled=True)
    return call(finish, (PER, V))(parts.reshape(rows, LANES))


def solution(mesh):
    n_row = mesh.shape["row"]
    split = Mesh(mesh.devices.reshape(n_row, N_YZ, 2), ("row", "yz", "core"))
    every = ("row", "yz", "core")
    return jax.shard_map(
        on_device,
        mesh=split,
        in_specs=(P(every, None), P("row", ("yz", "core"))),
        out_specs=P(every, None),
        check_vma=False,
    )
```

```python
import jax
import jax.numpy as jnp
from jax import lax
from jax.experimental import pallas as pl
from jax.experimental.pallas import tpu as pltpu
from jax.sharding import Mesh, PartitionSpec as P

O = 40
V = 512
LANES = 128
PER = 4
DEPTH = PER * O
REST = DEPTH - LANES
DEVICES = V // PER
CHIPS = DEVICES // 2
ROWS_OUT = PER * V // LANES
CHUNK = 40
N_YZ = 8
FAR = (0, 4)

NEAR_ORDER = (2, 3, 1)

VMEM = pltpu.VMEM
F32 = jnp.float32


def call(body, out_shapes, scratch=(), flops=0, moved=1 << 20, **specs):
    several = isinstance(out_shapes, list)
    outs = [
        s if isinstance(s, jax.ShapeDtypeStruct) else jax.ShapeDtypeStruct(s, F32)
        for s in (out_shapes if several else [out_shapes])
    ]
    return pl.pallas_call(
        body,
        out_shape=outs if several else outs[0],
        scratch_shapes=list(scratch),
        **specs,
        cost_estimate=pl.CostEstimate(flops=flops, bytes_accessed=moved, transcendentals=0),
        compiler_params=pltpu.CompilerParams(vmem_limit_bytes=16 << 20),
    )


def lane_index(rows):
    return lax.broadcasted_iota(jnp.int32, (rows, LANES), 1)


def rolled(x, shift):
    shift %= LANES
    return x if shift == 0 else pltpu.roll(x, shift, 1)


def window(parts, start, rows):
    first, off = divmod(start, LANES)
    if off == 0:
        return parts(first)
    low, high = rolled(parts(first), -off), rolled(parts(first + 1), -off)
    return jnp.where(lane_index(rows) < LANES - off, low, high)


def chunk(n):
    return pl.ds(CHUNK * n if isinstance(n, int) else pl.multiple_of(CHUNK * n, 8), CHUNK)


def pack_multiplier(m_ref, out_ref):
    groups = DEVICES // 4
    lane = lane_index(groups)
    for j in range(4):
        rest = None
        for i in range(PER):
            piece = lambda n, i=i: m_ref[pl.ds(4 * n + i, groups, stride=20), :]
            out_ref[pl.ds(5 * j + i, groups, stride=20), :] = window(piece, DEPTH * j, groups)
            tail = rolled(piece(j + 1), REST * (i - j))
            rest = tail if rest is None else jnp.where(lane >= REST * i, tail, rest)
        out_ref[pl.ds(5 * j + 4, groups, stride=20), :] = rest


def pack_swapped(m_ref, out_ref):
    groups = DEVICES // 4
    lane = lane_index(groups)
    for j in range(4):
        rest = None
        for i in range(PER):
            u = 4 * j + i
            main = None
            for c in range(PER):
                piece = lambda n, c=c: m_ref[pl.ds(4 * n + c, groups, stride=20), :]
                first, off = divmod(O * u, LANES)
                block = piece(first)
                if off + O > LANES:
                    block = jnp.where(lane >= off, block, piece(first + 1))
                at = O * c
                block_main = rolled(block, at - off)
                main = block_main if main is None else jnp.where(lane >= at, block_main, main)
                if at + O > LANES:
                    keep = LANES - at
                    tail = rolled(block, REST * i - off - keep)
                    rest = tail if rest is None else jnp.where(lane >= REST * i, tail, rest)
            out_ref[pl.ds(5 * j + i, groups, stride=20), :] = main
        out_ref[pl.ds(5 * j + 4, groups, stride=20), :] = rest


def pack_cycle(w_hbm, m_hbm, own_ref, other_ref, m_ref, w_ref, all_ref, sems):
    w_copy = pltpu.make_async_copy(w_hbm, w_ref, sems.at[0])
    m_copy = pltpu.make_async_copy(m_hbm, m_ref, sems.at[1])
    w_copy.start()
    m_copy.start()
    w_copy.wait()
    rest = [None] * (2 * N_YZ)
    lane = lane_index(8)
    for g in range(PER):
        for e in range(2 * N_YZ):
            piece = lambda n, g=g: w_ref[8 * g : 8 * g + 8, LANES * n : LANES * n + LANES]
            all_ref[CHUNK * e + 8 * g : CHUNK * e + 8 * g + 8, :] = window(piece, DEPTH * e, 8)
            first, off = divmod(DEPTH * e + LANES, LANES)
            tail = rolled(piece(first), REST * g - off)
            rest[e] = tail if g == 0 else jnp.where(lane >= REST * g, tail, rest[e])
    for e in range(2 * N_YZ):
        all_ref[CHUNK * e + 32 : CHUNK * e + 40, :] = rest[e]
    core = lax.axis_index("core")
    for yz in range(N_YZ):
        own_ref[chunk(yz), :] = all_ref[chunk(2 * yz + core), :]
        other_ref[chunk(yz), :] = all_ref[chunk(2 * yz + 1 - core), :]
    m_copy.wait()


def turn_far(own_ref, other_ref, *out_refs):
    me = lax.axis_index("yz")
    for k, ref in zip(FAR, out_refs):
        for z in range(4):
            for s, came in enumerate((own_ref, other_ref)):
                ref[chunk(2 * z + s), :] = came[chunk(((me ^ k) & 4) + z), :]


def turn_near(*refs):
    came, out_refs = refs[: len(FAR)], refs[len(FAR) :]
    z = lax.axis_index("yz") & 3
    for j, ref in enumerate(out_refs):
        for n, piece in enumerate(came):
            for s in range(2):
                ref[chunk(2 * n + s), :] = piece[chunk(2 * (z ^ j) + s), :]


def split(x):
    high = x.astype(jnp.bfloat16)
    return high, (x - high.astype(F32)).astype(jnp.bfloat16)


def rest_side(x, y, swapped):
    lane = lane_index(x.shape[0])
    both = jnp.where(lane < REST, x, rolled(y, REST))
    high, low = split(jnp.where(lane < 2 * REST, both, 0.0))
    wide = high.astype(F32), low.astype(F32)
    first, second = (wide[0], wide[0]) if swapped else wide
    third = low if swapped else high
    return [(first + rolled(second, LANES // 2)).astype(jnp.bfloat16), third]


def left_side(slab, cycle, slab_rest, cycle_rest):
    (a, a_low), (w, w_low) = split(slab), split(cycle)
    return jnp.concatenate([a, a_low, w, w_low, a, w, *rest_side(slab_rest, cycle_rest, False)], axis=1)


def right_side(cycle, slab, cycle_rest, slab_rest):
    (w, w_low), (a, a_low) = split(cycle), split(slab)
    return jnp.concatenate([w, w, a, a, w_low, a_low, *rest_side(cycle_rest, slab_rest, True)], axis=1)


def half_update(p_ref, q_ref, out_ref):
    term = lax.dot_general(
        p_ref[...], q_ref[...], (((1,), (1,)), ((), ())), preferred_element_type=F32
    )
    for i in range(PER):
        for m in range(V // LANES):
            piece = term[CHIPS * i : CHIPS * i + CHIPS, LANES * m : LANES * m + LANES]
            out_ref[pl.ds(4 * m + i, CHIPS, stride=ROWS_OUT), :] = piece


def arrange_slab(got_ref, swapped_ref, by_core_ref, by_row_ref, x_ref):
    core = lax.axis_index("core")
    x_ref[...] = 2.0 * got_ref[...] - swapped_ref[...]
    for h, parity in enumerate((1 - core, core)):
        packed = x_ref[pl.ds(5 * parity + 4, CHIPS, stride=10), :]
        for i in range(PER):
            parts = x_ref[pl.ds(5 * parity + i, CHIPS, stride=10), :], rolled(packed, -REST * i)
            for n, part in enumerate(parts):
                by_core_ref[n, h, CHIPS * i : CHIPS * i + CHIPS, :] = part
                by_row_ref[n, pl.ds(4 * parity + i, CHIPS, stride=8), :] = part


def first_half(a_core, a_row, w0, w1, w2, w3, out_ref, w_core, q_ref, w_ref, w_row, p_ref):
    me, core = lax.axis_index("yz"), lax.axis_index("core")
    for j, ref in enumerate((w0, w1, w2, w3)):
        for n, k in enumerate(FAR):
            for s in range(2):
                w_ref[chunk(2 * (me ^ k ^ j) + (core ^ s)), :] = ref[chunk(2 * n + s), :]
    n_row = DEVICES // (2 * N_YZ)
    for h, parity in enumerate((1 - core, core)):
        for i in range(PER):
            for r in range(n_row):
                first = CHUNK * parity + 4 * r + i, CHUNK * parity + 32 + 4 * (r % 2) + i
                for n, at in enumerate(first):
                    part = w_ref[pl.ds(at, N_YZ, stride=2 * CHUNK), :]
                    part = rolled(part, -REST * (r // 2)) if n else part
                    begin = CHIPS * i + N_YZ * r
                    w_core[n, h, begin : begin + N_YZ, :] = part
                    w_row[n, pl.ds(8 * N_YZ * r + 4 * parity + i, N_YZ, stride=8), :] = part

    q_ref[...] = right_side(w_row[0], a_row[0], w_row[1], a_row[1])
    p_ref[...] = left_side(a_core[0, 0], w_core[0, 0], a_core[1, 0], w_core[1, 0])
    half_update(p_ref, q_ref, out_ref)


def second_half(a_core, w_core, q_ref, out_ref, p_ref):
    p_ref[...] = left_side(a_core[0, 1], w_core[0, 1], a_core[1, 1], w_core[1, 1])
    half_update(p_ref, q_ref, out_ref)


def finish(parts_ref, out_ref):
    total = parts_ref[0:ROWS_OUT, :]
    for n in range(1, parts_ref.shape[0] // ROWS_OUT):
        total += parts_ref[ROWS_OUT * n : ROWS_OUT * n + ROWS_OUT, :]
    for m in range(V // LANES):
        out_ref[:, LANES * m : LANES * m + LANES] = total[4 * m : 4 * m + 4, :]


def swap(x, axis, k):
    return lax.ppermute(x, axis, [(n, n ^ k) for n in range(lax.axis_size(axis))])


def on_device(multiplier, cycle_tiles):
    slab = multiplier.reshape(PER, DEPTH, LANES).transpose(1, 0, 2).reshape(PER * DEPTH, LANES)
    half, quarter = (N_YZ * CHUNK, LANES), (4 * CHUNK, LANES)
    columns = cycle_tiles.T
    own, other, slab = call(
        pack_cycle,
        [half, half, slab.shape],
        scratch=[
            VMEM(columns.shape, F32),
            VMEM((2 * N_YZ * CHUNK, LANES), F32),
            pltpu.SemaphoreType.DMA((2,)),
        ],
        in_specs=[pl.BlockSpec(memory_space=pltpu.HBM)] * 2,
        out_specs=[pl.BlockSpec(memory_space=VMEM)] * 3,
    )(*(pltpu.with_memory_space_constraint(x, pltpu.HBM) for x in (columns, slab)))
    other = swap(other, "core", 1)
    packed = call(pack_multiplier, (5 * DEVICES, LANES))(slab)
    far = call(turn_far, [half] * 2)(own, other)
    far = [far[0], *(swap(x, "yz", k) for k, x in zip(FAR[1:], far[1:]))]
    got = lax.all_to_all(
        packed.reshape(DEVICES, 1, 5 * LANES), ("row", "yz", "core"), 0, 0, tiled=True
    )
    near = list(call(turn_near, [quarter] * 4)(*far))
    for j in NEAR_ORDER:
        near[j] = swap(near[j], "yz", j)
    swapped = call(pack_swapped, (5 * DEVICES, LANES))(slab)
    width = 8 * LANES
    rows, flops = CHIPS * ROWS_OUT, V * V * width
    by_core, by_row = (2, 2, V // 2, LANES), (2, V, LANES)
    a_core, a_row = call(arrange_slab, [by_core, by_row], scratch=[VMEM((5 * DEVICES, LANES), F32)])(
        got.reshape(5 * DEVICES, LANES), swapped
    )
    left = VMEM((V // 2, width), jnp.bfloat16)
    theirs, w_core, q = call(
        first_half,
        [(rows, LANES), by_core, jax.ShapeDtypeStruct((V, width), jnp.bfloat16)],
        scratch=[VMEM((2 * N_YZ * CHUNK, LANES), F32), VMEM(by_row, F32), left],
        flops=flops,
    )(a_core, a_row, *near)
    theirs = swap(theirs, "core", 1)
    mine = call(second_half, (rows, LANES), scratch=[left], flops=flops)(a_core, w_core, q)
    share = mine + theirs
    parts = lax.all_to_all(share.reshape(CHIPS, ROWS_OUT, LANES), ("row", "yz"), 0, 0, tiled=True)
    return call(finish, (PER, V))(parts.reshape(rows, LANES))


def solution(mesh):
    n_row = mesh.shape["row"]
    split = Mesh(mesh.devices.reshape(n_row, N_YZ, 2), ("row", "yz", "core"))
    every = ("row", "yz", "core")
    return jax.shard_map(
        on_device,
        mesh=split,
        in_specs=(P(every, None), P("row", ("yz", "core"))),
        out_specs=P(every, None),
        check_vma=False,
    )
```
